256 devices in a mesh: lat: 16 (over y_lo, x, core), lon: 16 (over z, y_hi).
Axes of the slice: x: 4, y: 4 (y_hi: 2, y_lo: 2; y = y_hi * 2 + y_lo), z: 8, core: 2. Of those that a mesh axis runs over, the one named last changes fastest.
Arguments:
- fields: bfloat16 [768, 2048, 128], P('lat', 'lon'), may hold values from -6 to 6
- wet_mask: int32 [768, 2048], P('lat', 'lon'), may hold values 0 or 1
- conv_kernel: float32 [2, 49, 128], replicated, may hold values from -0.875 to 0.875
- conv_bias: float32 [2, 128], replicated, may hold values from -3 to 3
- norm_gain: float32 [2, 128], replicated, may hold values from 0.5 to 1.5
- norm_bias: float32 [2, 128], replicated, may hold values from -2 to 2
- in_weight: bfloat16 [2, 128, 512], replicated, may hold values from -0.5 to 0.5
- in_bias: float32 [2, 512], replicated, may hold values from -3 to 3
- out_weight: bfloat16 [2, 512, 128], replicated, may hold values from -0.25 to 0.25
- out_bias: float32 [2, 128], replicated, may hold values from -2 to 2
- layer_scale: float32 [2, 128], replicated, may hold values from 0.5 to 1.5
Outputs:
- result: bfloat16 [768, 2048, 128], P('lat', 'lon')
The draws below stay inside these ranges and needn't reach their ends.
Inputs may be any that keep to these rules, and one draw needn't show every extreme that they name: wet_mask holds only 0 and 1.
All inputs are finite; a program needn't handle non-finite values. No bound on the sum of `wet_mask` on one device may be relied on, other than what follows from the above.
Results may differ from the reference program's by a relative error of at most 0.0057.
Values may be sent and summed in bfloat16 or wider, within the bound.
A program may use at most 64 MiB of HBM per device.

```python
import jax
import jax.numpy as jnp
from jax import lax

C = 128
HID = 512
RD = 48
H = 768
W = 2048


def with_ends(drawn, stream_key, smallest, high):
    longest = drawn.shape.index(max(drawn.shape))
    spots = []
    for shift in (0, 1):
        where = [jax.random.randint(jax.random.fold_in(stream_key, axis), (), 0, length) for axis, length in enumerate(drawn.shape)]
        where[longest] = (where[longest] + shift) % drawn.shape[longest]
        spots.append(tuple(where))
    return drawn.at[spots[0]].set(smallest).at[spots[1]].set(high)


def block_levels(own_key, dims, shards, smallest, top_value):
    def one(axis_at, parts):
        heights = jax.random.uniform(jax.random.fold_in(jax.random.fold_in(own_key, 6), axis_at), (parts,), jnp.float32, smallest / len(shards), top_value / len(shards))
        return jnp.repeat(jnp.exp(heights), dims[axis_at] // parts).reshape((-1,) + (1,) * (len(dims) - axis_at - 1))

    level = one(*shards[0])
    for cut in shards[1:]:
        level = level * one(*cut)
    return level


def bell_draw(rng, extent, spread, bound, split=(), held_as=jnp.bfloat16):
    loudness = block_levels(rng, extent, split, -0.22, 0.18) if split else 1.0
    array = jax.random.normal(rng, extent, jnp.float32) * spread * loudness
    return jnp.minimum(jnp.maximum(array, -bound), bound).astype(held_as)


def setup_inputs(seed: int = 0) -> dict:
    key_list = jax.random.split(jax.random.key(seed), 12)
    return {
        "fields": bell_draw(key_list[0], (H, W, C), 1.0, 6.0, ((0, 16), (1, 16))),
        "wet_mask": with_ends((jax.random.randint(key_list[1], (H, W), 0, 4) < 3).astype(jnp.int32), jax.random.fold_in(key_list[1], 1), 0, 1),
        "conv_kernel": bell_draw(key_list[2], (2, 49, C), 49 ** -0.5, 0.875, (), jnp.float32),
        "conv_bias": bell_draw(key_list[3], (2, C), 0.5, 3.0, (), jnp.float32),
        "norm_gain": jnp.clip(1.0 + 0.1 * jax.random.normal(key_list[4], (2, C), jnp.float32), 0.5, 1.5),
        "norm_bias": bell_draw(key_list[5], (2, C), 0.3, 2.0, (), jnp.float32),
        "in_weight": bell_draw(key_list[6], (2, C, HID), C ** -0.5, 0.5),
        "in_bias": bell_draw(key_list[7], (2, HID), 0.5, 3.0, (), jnp.float32),
        "out_weight": bell_draw(key_list[8], (2, HID, C), HID ** -0.5, 0.25),
        "out_bias": bell_draw(key_list[9], (2, C), 0.3, 2.0, (), jnp.float32),
        "layer_scale": jnp.clip(1.0 + 0.1 * jax.random.normal(key_list[10], (2, C), jnp.float32), 0.5, 1.5),
    }


def pad_grid(values):
    ext = jnp.concatenate([values[:, -3:], values, values[:, :3]], axis=1)
    south = jnp.zeros((3,) + ext.shape[1:], ext.dtype)
    north = ext[-3:][::-1, ::-1]
    return jnp.concatenate([south, ext, north], axis=0)

def block_rows(band, residual, index, conv_kernel, conv_bias, norm_gain, norm_bias, in_weight, in_bias, out_weight, out_bias, layer_scale):
    rows = residual.shape[0]
    cols = residual.shape[1]
    acc = jnp.zeros((rows, cols, band.shape[2]), jnp.float32)
    for row_tap in range(7):
        for col_tap in range(7):
            acc = acc + band[row_tap:row_tap + rows, col_tap:col_tap + cols].astype(jnp.float32) * conv_kernel[index, 7 * row_tap + col_tap]
    acc = acc + conv_bias[index]
    mean = lax.optimization_barrier(jnp.mean(acc, axis=-1, keepdims=True))
    var = lax.optimization_barrier(jnp.mean((acc - mean) ** 2, axis=-1, keepdims=True))
    normed = ((acc - mean) * lax.rsqrt(var + 1e-06) * norm_gain[index] + norm_bias[index]).astype(jnp.bfloat16)
    flat = normed.reshape(rows * cols, -1)
    hidden = jnp.dot(flat, in_weight[index], preferred_element_type=jnp.float32) + in_bias[index]
    hidden = jax.nn.gelu(hidden, approximate=False).astype(jnp.bfloat16)
    branch = jnp.dot(hidden, out_weight[index], preferred_element_type=jnp.float32) + out_bias[index]
    branch = branch * layer_scale[index]
    return (residual.astype(jnp.float32) + branch.reshape(rows, cols, -1)).astype(jnp.bfloat16)

def reference(fields, wet_mask, conv_kernel, conv_bias, norm_gain, norm_bias, in_weight, in_bias, out_weight, out_bias, layer_scale):
    mask_bf = wet_mask.astype(jnp.bfloat16)
    state = fields * mask_bf[:, :, None]
    bands = H // RD
    for index in range(2):
        padded = pad_grid(state)

        def one_band(band_index):
            start = (band_index * RD).astype(jnp.int32)
            band = lax.dynamic_slice_in_dim(padded, start, RD + 6, 0)
            residual = lax.dynamic_slice_in_dim(state, start, RD, 0)
            return block_rows(band, residual, index, conv_kernel, conv_bias, norm_gain, norm_bias, in_weight, in_bias, out_weight, out_bias, layer_scale)
        state = lax.map(one_band, jnp.arange(bands, dtype=jnp.int32)).reshape(H, W, -1)
    return state * mask_bf[:, :, None]
```

```python
import jax, jax.numpy as jnp, functools
from jax import lax
from jax.experimental import pallas as pl
from jax.experimental.pallas import tpu as pltpu
from jax.sharding import PartitionSpec as P
BF=jnp.bfloat16; F=jnp.float32
R=4
def iota(s,d): return lax.broadcasted_iota(jnp.int32,s,d)
def dot(a,b): return jnp.dot(a,b,preferred_element_type=F)
def tree(v):
    while len(v)>1:
        v=[v[i]+v[i+1] if i+1<len(v) else v[i] for i in range(0,len(v),2)]
    return v[0]
def conv_row(XG, KF, bias, C, row, at):
    acc=[bias]*8
    for r in range(7):
        xs=[XG[row+r,k] for k in range(14)]
        ws=[]
        for s in range(7):
            w=KF[7*r+s]
            ws.append(jnp.concatenate([w,w],0).astype(BF))
        for k in range(8):
            acc[k]=acc[k]+tree([ws[s]*xs[k+s] for s in range(7)]).astype(F)
    for k in range(8):
        C[at*128+k*16:at*128+k*16+16,:]=acc[k]
def mlp_rows(C, XG, Y, row0, W1E, W2, VM, gain, nb, b2, ls):
    M=R*128
    c=C[...]
    cen=c-dot(c.astype(BF),VM)
    var=dot((cen*cen).astype(BF),VM)
    normed=(cen*lax.rsqrt(var+1e-6)*gain+nb).astype(BF)
    ones=jnp.where(iota((M,128),1)<3,1.0,0.0).astype(BF)
    t=dot(jnp.concatenate([normed,ones],1),W1E[...])
    g=(t*lax.erf(t*1.4142135623730951)+t).astype(BF)
    y=(dot(g,W2[...])+b2)*ls
    for rr in range(R):
        for k in range(8):
            res=XG[row0+rr+3,k+3].astype(F)
            Y[row0+rr,k]=(res+y[rr*128+k*16:rr*128+k*16+16]).astype(BF)
def kernel(idx, st, south, north, side, CK, cb, gain, nb, W1, b1, W2, b2, ls, out, XG, KF, W1E, W2S, C0, C1, Y):
    def src_matrix():
        n=iota((224,144),0); c=iota((224,144),1)
        col=8*(n%16)+n//16
        src=jnp.where(col<3,128+col,jnp.where(col>=131,col,col-3))
        return jnp.where(src==c,1.0,0.0).astype(BF)
    G=src_matrix()
    n=iota((128,128),0); c=iota((128,128),1)
    U=jnp.where((n%8)*16+n//8==c,1.0,0.0).astype(BF)
    VM=jnp.full((128,128),1/128,BF)
    for t in range(49):
        KF[t]=jnp.broadcast_to(CK[idx,t:t+1,:],(8,128))
    W1E[:128]=W1[idx]*BF(0.5)
    bb=b1[idx:idx+1]*0.5
    hi=bb.astype(BF).astype(F); lo=(bb-hi).astype(BF).astype(F); l2=bb-hi-lo
    z=iota((128,512),0)
    W1E[128:]=jnp.where(z==0,hi,jnp.where(z==1,lo,jnp.where(z==2,l2,0.0))).astype(BF)
    W2S=W2.at[idx]
    def put(i,mid,sd):
        XG[i]=dot(G,jnp.concatenate([mid,sd],0)).astype(BF).reshape(14,16,128)
    def prep(i,c):
        put(i+3,st[i],side[i+3]); return c
    lax.fori_loop(0,48,prep,0,unroll=2)
    for i in range(3):
        put(i,south[i],side[i]); put(51+i,north[i],side[51+i])
    bias=jnp.broadcast_to(cb[idx:idx+1],(16,128))
    def A(C,row0):
        for rr in range(R): conv_row(XG,KF,bias,C,row0+rr,rr)
    B=lambda Cx,row0: mlp_rows(Cx,XG,Y,row0,W1E,W2S,VM,gain[idx:idx+1],nb[idx:idx+1],b2[idx:idx+1],ls[idx:idx+1])
    n=48//R
    A(C0,0)
    def body(j,c):
        r0=j*2*R
        B(C0,r0); A(C1,r0+R)
        B(C1,r0+R); A(C0,r0+2*R)
        return c
    lax.fori_loop(0,n//2-1,body,0)
    r0=(n-2)*R
    B(C0,r0); A(C1,r0+R)
    B(C1,r0+R)
    def fin(i,c):
        out[i]=dot(U,Y[i].reshape(128,128)).astype(BF)
        return c
    lax.fori_loop(0,48,fin,0,unroll=2)
def block(idx, st, south, north, side, *w):
    vm=pl.BlockSpec(memory_space=pltpu.VMEM)
    return pl.pallas_call(functools.partial(kernel,idx),out_shape=jax.ShapeDtypeStruct((48,128,128),BF),
      in_specs=[vm]*13,out_specs=vm,
      scratch_shapes=[pltpu.VMEM((54,14,16,128),BF),pltpu.VMEM((49,8,128),F),pltpu.VMEM((256,512),BF),pltpu.VMEM((8,128),F),pltpu.VMEM((R*128,128),F),pltpu.VMEM((R*128,128),F),pltpu.VMEM((48,8,16,128),BF)],
      compiler_params=pltpu.CompilerParams(vmem_limit_bytes=60<<20),
      cost_estimate=pl.CostEstimate(flops=2*10**9,bytes_accessed=4*10**6,transcendentals=0),
      name=f"block{idx}",
    )(st,south,north,side,*w)

def halos(state):
    n = lax.axis_size("lon"); m = lax.axis_size("lat")
    up = [(i, (i + 1) % n) for i in range(n)]
    left = lax.ppermute(state[:, -3:], "lon", up)
    right = lax.ppermute(state[:, :3], "lon", [(j, i) for i, j in up])
    side = jnp.concatenate([left, right], 1)
    top = jnp.concatenate([state[-3:], side[-3:]], 1)
    bot = jnp.concatenate([state[:3], side[:3]], 1)
    south = lax.ppermute(top, "lat", [(i, i + 1) for i in range(m - 1)])
    ext = jnp.concatenate([top[:, 128:131], top[:, :128], top[:, 131:]], 1)[::-1, ::-1]
    fold = jnp.concatenate([ext[:, 3:131], ext[:, :3], ext[:, 131:]], 1)
    is_top = lax.axis_index("lat") == m - 1
    north = lax.ppermute(bot, "lat", [(i + 1, i) for i in range(m - 1)])
    route = [((m - 1) * n + l, (m - 1) * n + n - 1 - l) for l in range(n)]
    fold = lax.ppermute(fold, ("lat", "lon"), route)
    north = jnp.where(is_top, fold, north)
    full = jnp.concatenate([south[:, 128:], side, north[:, 128:]], 0)
    full = jnp.pad(full, ((0, 0), (0, 10), (0, 0)))
    return south[:, :128], north[:, :128], full
def shards(fields, wet_mask, *w):
    mask_bf = wet_mask.astype(BF)[:, :, None]
    state = fields * mask_bf
    for index in range(2):
        south, north, side = halos(state)
        state = block(index, state, south, north, side, *w)
    return state * mask_bf
def solution(mesh):
    return jax.shard_map(shards, mesh=mesh, in_specs=(P("lat", "lon", None), P("lat", "lon")) + (P(),) * 9,
        out_specs=P("lat", "lon", None), check_vma=False)
```

```python
import functools

import jax
import jax.numpy as jnp
from jax import lax
from jax.experimental import pallas as pl
from jax.experimental.pallas import tpu as pltpu
from jax.sharding import PartitionSpec as P

BF, F = jnp.bfloat16, jnp.float32
R = 4
ROWS, COLS, C = 48, 128, 128
N = ROWS // R
MESH = pl.DeviceIdType.MESH


def iota(shape, d):
    return lax.broadcasted_iota(jnp.int32, shape, d)


def onehot(cond):
    return jnp.where(cond, 1.0, 0.0).astype(BF)


def dot(a, b):
    return jnp.dot(a, b, preferred_element_type=F)


def tree(v):
    while len(v) > 1:
        v = [v[i] + v[i + 1] if i + 1 < len(v) else v[i] for i in range(0, len(v), 2)]
    return v[0]


def chunk0(s):
    return jnp.where(s < 8, s + 1, jnp.where(s == 8, 0, jnp.where(s == 9, 11, s - 1)))


def chunk1(s):
    return jnp.where(s < 7, s + 2, jnp.where(s == 7, 1, jnp.where(s < 10, s + 1, (s - 10) * 11)))


def conv(XG, KF, bias, acc_ref, row0):
    for rr in range(R):
        acc = [bias] * 8
        for r in range(7):
            xs = [XG[row0 + rr + r, k] for k in range(14)]
            ws = []
            for s in range(7):
                w = KF[7 * r + s]
                ws.append(jnp.concatenate([w, w], 0).astype(BF))
            for k in range(8):
                acc[k] = acc[k] + tree([ws[s] * xs[k + s] for s in range(7)]).astype(F)
        for k in range(8):
            acc_ref[rr * 128 + k * 16 : rr * 128 + k * 16 + 16, :] = acc[k]


def mlp(acc_ref, VM, W1E, W2, gain, nb, b2, ls):
    c = acc_ref[...]
    cen = c - dot(c.astype(BF), VM)
    var = dot((cen * cen).astype(BF), VM)
    normed = (cen * lax.rsqrt(var + 1e-6) * gain + nb).astype(BF)
    ones = onehot(iota((R * 128, 128), 1) < 3)
    t = dot(jnp.concatenate([normed, ones], 1), W1E[...])
    g = (t * lax.erf(t * 1.4142135623730951) + t).astype(BF)
    return (dot(g, W2[...]) + b2) * ls


def kernel(
    fields, mask, CK, cb, gain, nb, W1, b1, W2, b2, ls, out,
    NAT, XG0, XG1, CKV, KF, W1V, W1E, W2V, G4, H4, INS, UM, MG,
    acc0, acc1, EL, ER, LH, RH, FB, load_sem, send_sem, recv_sem, out_sem,
):
    lat, lon = lax.axis_index("lat"), lax.axis_index("lon")
    nlat, nlon = lax.axis_size("lat"), lax.axis_size("lon")
    right, left = lax.rem(lon + 1, nlon), lax.rem(lon + nlon - 1, nlon)
    fold = nlon - 1 - lon
    is_top, is_low = lat == nlat - 1, lat == 0
    not_top, not_low = lat < nlat - 1, lat > 0

    loads = [pltpu.make_async_copy(fields.at[pl.ds(12 * q, 12)], NAT.at[pl.ds(12 * q, 12)], load_sem.at[q]) for q in range(4)]
    loads += [
        pltpu.make_async_copy(CK, CKV, load_sem.at[4]),
        pltpu.make_async_copy(W1, W1V, load_sem.at[5]),
        pltpu.make_async_copy(W2, W2V, load_sem.at[6]),
    ]
    for cp in loads:
        cp.start()

    barrier = pltpu.get_barrier_semaphore()

    def greet(a, o):
        pl.semaphore_signal(barrier, inc=1, device_id={"lat": a, "lon": o}, device_id_type=MESH)

    greet(lat, left)
    greet(lat, right)

    @pl.when(not_low)
    def _():
        greet(lat - 1, lon)

    @pl.when(not_top)
    def _():
        greet(lat + 1, lon)

    @pl.when(is_top)
    def _():
        greet(lat, fold)

    def remote(src, dst, i, j, a, o):
        return pltpu.make_async_remote_copy(
            src_ref=src, dst_ref=dst, send_sem=send_sem.at[i], recv_sem=recv_sem.at[j],
            device_id={"lat": a, "lon": o}, device_id_type=MESH,
        )

    n, c = iota((256, 128), 0), iota((256, 128), 1)
    col = 8 * (n % 16) + n // 16 - 3
    h, hc = iota((128, 128), 0), iota((128, 128), 1)
    kk = h // 16
    g16 = h % 16
    ksrc = jnp.where(kk < 3, kk + 5, kk - 3)
    gsrc = jnp.where(kk < 3, g16 - 1, g16 + 1)
    hsrc = jnp.where((gsrc >= 0) & (gsrc < 16), ksrc * 16 + gsrc, -1)
    for rr in range(R):
        e = g16 - 4 * rr
        ok = (e >= 0) & (e < 3)
        en = n % 16 - 4 * rr
        okn = (en >= 0) & (en < 3)
        lsrc, rsrc = jnp.where(okn, en, -1), jnp.where(okn, 125 + en, -1)
        G4[rr] = onehot(jnp.where(n < 224, col, jnp.where(n < 240, lsrc, rsrc)) == c)
        hl, hr = jnp.where(ok, e * 16, -1), jnp.where(ok, (5 + e) * 16 + 15, -1)
        H4[rr] = onehot(jnp.where(kk < 6, hsrc, jnp.where(kk < 7, hl, hr)) == hc)
    m, mc = iota((96 * R, 32), 0), iota((96 * R, 32), 1)
    mr, mk, mg = m // 96, (m % 96) // 16, m % 16
    INS[...] = onehot(jnp.where(mk < 3, jnp.where(mg == 0, 4 * mr + mk, -1), jnp.where(mg == 15, 13 + 4 * mr + mk, -1)) == mc)
    UM[...] = onehot((h % 8) * 16 + h // 8 == hc)
    MG[...] = dot(mask[...].astype(F).astype(BF), onehot((hc % 16) * 8 + hc // 16 == h))
    VM = jnp.full((128, 128), 1 / 128, BF)

    def pairs(b, lo, hi, base):
        a, z = 16 * lo, 16 * (hi - lo)
        return (
            remote(ER.at[b, pl.ds(a, z)], LH.at[b, pl.ds(a, z)], base, base, lat, right),
            remote(EL.at[b, pl.ds(a, z)], RH.at[b, pl.ds(a, z)], base + 1, base + 1, lat, left),
        )

    cols0 = pairs(0, 0, 12, 0)
    colsA = pairs(1, 1, 9, 2)
    colsB = pairs(1, 0, 1, 4)
    colsC = pairs(1, 11, 12, 6)
    colsD = pairs(1, 9, 11, 8)
    cols1 = colsA + colsB + colsC + colsD

    def rows(XG, b):
        i = 10 + 3 * b
        north = remote(XG.at[pl.ds(48, 3)], XG.at[pl.ds(0, 3)], i, i, lat + 1, lon)
        across = remote(XG.at[pl.ds(48, 3)], FB.at[b], i + 1, i + 1, lat, fold)
        south = remote(XG.at[pl.ds(3, 3)], XG.at[pl.ds(51, 3)], i + 2, i + 2, lat - 1, lon)
        return north, across, south

    rows0, rows1 = rows(XG0, 0), rows(XG1, 1)

    def send_rows(copies):
        north, across, south = copies
        pl.when(not_top)(north.start)
        pl.when(is_top)(across.start)
        pl.when(not_low)(south.start)

    def wait_rows(XG, b, copies):
        north, across, south = copies
        pl.when(not_low)(north.wait_recv)

        @pl.when(is_low)
        def _():
            XG[0:3] = jnp.zeros((3, 14, 16, 128), BF)

        pl.when(not_top)(south.wait_recv)

        @pl.when(is_top)
        def _():
            across.wait_recv()
            flip = onehot(iota((224, 224), 0) + iota((224, 224), 1) == 223)
            for j in range(3):
                XG[51 + j] = dot(flip, FB[b, 2 - j].reshape(224, 128)).astype(BF).reshape(14, 16, 128)

    def insert(XG, b, ch):
        at = pl.ds(pl.multiple_of(16 * ch, 16), 16)
        o = dot(INS[...], jnp.concatenate([LH[b, at], RH[b, at]], 0)).astype(BF)
        for rr in range(R):
            row = R * ch + rr + 3
            XG[row, 0:3] = XG[row, 0:3] + o[rr * 96 : rr * 96 + 48].reshape(3, 16, 128)
            XG[row, 11:14] = XG[row, 11:14] + o[rr * 96 + 48 : rr * 96 + 96].reshape(3, 16, 128)

    def edges(b, ch, el, er):
        at = pl.ds(pl.multiple_of(16 * ch, 16), 16)
        EL[b, at] = el.astype(BF)
        ER[b, at] = er.astype(BF)

    def prep(ch, carry):
        el = er = None
        for rr in range(R):
            row = R * ch + rr
            mrow = jnp.broadcast_to(mask[pl.ds(row, 1), :].astype(F), (16, 128)).astype(BF)
            lhs = (G4[rr].reshape(16, 16, 128) * mrow[None]).reshape(256, 128)
            o = dot(lhs, NAT[row])
            XG0[row + 3] = o[:224].astype(BF).reshape(14, 16, 128)
            el = o[224:240] if el is None else el + o[224:240]
            er = o[240:256] if er is None else er + o[240:256]
        edges(0, ch, el, er)
        return carry

    for q in range(4):
        loads[q].wait()
        lax.fori_loop(3 * q, 3 * q + 3, prep, 0)

    @pl.when(not_low & not_top)
    def _():
        pl.semaphore_wait(barrier, 4)

    @pl.when(is_low)
    def _():
        pl.semaphore_wait(barrier, 3)

    @pl.when(is_top)
    def _():
        pl.semaphore_wait(barrier, 4)

    for cp in cols0:
        cp.start()
    for cp in loads[4:]:
        cp.wait()
    for b in range(2):
        for t in range(49):
            KF[b, t] = jnp.broadcast_to(CKV[b, t : t + 1, :], (8, 128))
        W1E[b, :128] = W1V[b] * BF(0.5)
        bb = b1[b : b + 1] * 0.5
        hi = bb.astype(BF).astype(F)
        lo = (bb - hi).astype(BF).astype(F)
        z = iota((128, 512), 0)
        W1E[b, 128:] = jnp.where(z == 0, hi, jnp.where(z == 1, lo, jnp.where(z == 2, bb - hi - lo, 0.0))).astype(BF)
    for cp in cols0:
        cp.wait_recv()

    def ins0(ch, carry):
        insert(XG0, 0, ch)
        return carry

    lax.fori_loop(0, N, ins0, 0)
    send_rows(rows0)

    def stage(b, XG):
        bias = jnp.broadcast_to(cb[b : b + 1], (16, 128))
        vec = [v[b : b + 1] for v in (gain, nb, b2, ls)]
        A = lambda acc, ch: conv(XG, KF.at[b], bias, acc, R * ch)

        def B(acc, ch):
            y = mlp(acc, VM, W1E.at[b], W2V.at[b], *vec)
            el = er = None
            for rr in range(R):
                row = R * ch + rr
                res = XG[row + 3, 3:11].reshape(128, 128).astype(F)
                x = (res + y[rr * 128 : rr * 128 + 128]).astype(BF)
                if b == 0:
                    XG1[row + 3, 3:11] = x.reshape(8, 16, 128)
                    o = dot(H4[rr], x)
                    XG1[row + 3, 0:3] = o[:48].astype(BF).reshape(3, 16, 128)
                    XG1[row + 3, 11:14] = o[48:96].astype(BF).reshape(3, 16, 128)
                    el = o[96:112] if el is None else el + o[96:112]
                    er = o[112:128] if er is None else er + o[112:128]
                else:
                    mrow = jnp.broadcast_to(MG[pl.ds(row, 1), :], (16, 128)).astype(BF)
                    lhs = (UM[...].reshape(8, 16, 128) * mrow[None]).reshape(128, 128)
                    NAT[row] = dot(lhs, x).astype(BF)
            if b == 0:
                edges(1, ch, el, er)

        return A, B

    A, B = stage(0, XG0)
    A(acc0, chunk0(0))

    def body0(j, carry):
        @pl.when(j == 3)
        def _():
            wait_rows(XG0, 0, rows0)

        B(acc0, chunk0(2 * j))
        A(acc1, chunk0(2 * j + 1))
        B(acc1, chunk0(2 * j + 1))
        A(acc0, chunk0(2 * j + 2))

        @pl.when(j == 3)
        def _():
            for cp in colsA:
                cp.start()

        @pl.when(j == 4)
        def _():
            for cp in colsB + colsC:
                cp.start()

        return carry

    lax.fori_loop(0, N // 2 - 1, body0, 0)
    B(acc0, chunk0(N - 2))
    A(acc1, chunk0(N - 1))
    B(acc1, chunk0(N - 1))
    for cp in colsD:
        cp.start()

    for cp in colsA:
        cp.wait_recv()

    def ins1(ch, carry):
        insert(XG1, 1, ch)
        return carry

    lax.fori_loop(1, 9, ins1, 0)
    A, B = stage(1, XG1)
    A(acc0, chunk1(0))

    def finish(ch):
        return pltpu.make_async_copy(NAT.at[pl.ds(R * ch, R)], out.at[pl.ds(R * ch, R)], out_sem.at[ch])

    def body1(j, carry):
        @pl.when(j == 1)
        def _():
            for cp in colsB + colsC + colsD:
                cp.wait_recv()
            insert(XG1, 1, 0)
            insert(XG1, 1, 11)
            insert(XG1, 1, 9)
            insert(XG1, 1, 10)
            send_rows(rows1)

        @pl.when(j == 4)
        def _():
            wait_rows(XG1, 1, rows1)

        B(acc0, chunk1(2 * j))
        A(acc1, chunk1(2 * j + 1))
        B(acc1, chunk1(2 * j + 1))
        A(acc0, chunk1(2 * j + 2))
        finish(chunk1(2 * j)).start()
        finish(chunk1(2 * j + 1)).start()
        return carry

    lax.fori_loop(0, N // 2 - 1, body1, 0)
    B(acc0, chunk1(N - 2))
    A(acc1, chunk1(N - 1))
    B(acc1, chunk1(N - 1))
    finish(chunk1(N - 2)).start()
    finish(chunk1(N - 1)).start()

    for cp in cols0 + cols1:
        cp.wait_send()
    for north, across, south in (rows0, rows1):
        pl.when(not_top)(north.wait_send)
        pl.when(is_top)(across.wait_send)
        pl.when(not_low)(south.wait_send)
    for ch in range(N):
        finish(ch).wait()


def shards(fields, wet_mask, *w):
    CK, cb, gain, nb, W1, b1, W2, b2, ls = w
    vm, hbm = pl.BlockSpec(memory_space=pltpu.VMEM), pl.BlockSpec(memory_space=pl.ANY)
    V = pltpu.VMEM
    return pl.pallas_call(
        kernel,
        out_shape=jax.ShapeDtypeStruct((ROWS, COLS, C), BF),
        in_specs=[hbm, vm, hbm, vm, vm, vm, hbm, vm, hbm, vm, vm],
        out_specs=hbm,
        scratch_shapes=[
            V((ROWS, COLS, C), BF), V((54, 14, 16, C), BF), V((54, 14, 16, C), BF),
            V((2, 49, C), F), V((2, 49, 8, C), F), V((2, 128, 512), BF), V((2, 256, 512), BF), V((2, 512, 128), BF),
            V((R, 256, 128), BF), V((R, 128, 128), BF), V((96 * R, 32), BF), V((128, 128), BF), V((ROWS, 128), F),
            V((R * 128, C), F), V((R * 128, C), F),
            V((2, 192, C), BF), V((2, 192, C), BF), V((2, 192, C), BF), V((2, 192, C), BF), V((2, 3, 14, 16, C), BF),
            pltpu.SemaphoreType.DMA((7,)), pltpu.SemaphoreType.DMA((16,)), pltpu.SemaphoreType.DMA((16,)), pltpu.SemaphoreType.DMA((N,)),
        ],
        compiler_params=pltpu.CompilerParams(vmem_limit_bytes=60 << 20, collective_id=0, has_side_effects=True),
        name="forecast",
    )(fields, wet_mask, *w)


def solution(mesh):
    return jax.shard_map(
        shards, mesh=mesh, in_specs=(P("lat", "lon", None), P("lat", "lon")) + (P(),) * 9,
        out_specs=P("lat", "lon", None), check_vma=False,
    )
```

```python
import functools

import jax
import jax.numpy as jnp
from jax import lax
from jax.experimental import pallas as pl
from jax.experimental.pallas import tpu as pltpu
from jax.sharding import PartitionSpec as P

BF, F = jnp.bfloat16, jnp.float32
R = 4
ROWS, COLS, C = 48, 128, 128
N = ROWS // R
MESH = pl.DeviceIdType.MESH
VMB = 60
TAIL = 8
HALF = 0.7071067811865476
SPAN = ((0, 12), (12, 26), (4, 10))


def iota(shape, d):
    return lax.broadcasted_iota(jnp.int32, shape, d)


def onehot(cond):
    return jnp.where(cond, 1.0, 0.0).astype(BF)


def dot(a, b):
    return jnp.dot(a, b, preferred_element_type=F)


def tree(v):
    while len(v) > 1:
        v = [v[i] + v[i + 1] if i + 1 < len(v) else v[i] for i in range(0, len(v), 2)]
    return v[0]


ORDER = ([1, 2, 3, 4, 5, 6, 7, 0, 11, 8, 9, 10], [2, 3, 4, 5, 6, 1, 7, 8, 9, 10, 0, 11])


def chunk(b, q):
    if isinstance(q, int):
        return ORDER[b][q]
    if b == 0:
        return jnp.where(q < 7, q + 1, jnp.where(q == 7, 0, jnp.where(q == 8, 11, q - 1)))
    return jnp.where(q < 5, q + 2, jnp.where(q == 5, 1, jnp.where(q < 10, q + 1, (q - 10) * 11)))


def gate(pieces, marks, lo, hi):
    if not marks:
        return jnp.concatenate(pieces, 0)
    n = len(pieces)
    return jnp.concatenate([p + marks[lo + i * (hi - lo) // n] for i, p in enumerate(pieces)], 0)


def conv(XG, KF, bias, acc_ref, row0):
    marks = []
    for rr in range(R):
        acc = [bias] * 8
        for r in range(7):
            xs = [XG[row0 + rr + r, k] for k in range(14)]
            ws = []
            for s in range(7):
                w = KF[7 * r + s]
                ws.append(jnp.concatenate([w, w], 0).astype(BF))
            for k in range(8):
                part = tree([ws[s] * xs[k + s] for s in range(7)])
                acc[k] = acc[k] + part.astype(F)
            marks.append(part * BF(0))
        for k in range(8):
            acc_ref[rr * 128 + k * 16 : rr * 128 + k * 16 + 16, :] = acc[k]
    return marks


def norm(acc_ref, out_ref, gain, nb):
    c = acc_ref[...]
    cen = c - jnp.sum(c, axis=-1, keepdims=True) * (1 / 128)
    var = jnp.sum(cen * cen, axis=-1, keepdims=True)
    out_ref[...] = (cen * lax.rsqrt(var + 128e-6) * gain + nb).astype(BF)


def expand_hidden(nrm_ref, hid_ref, W1E, marks):
    ones = onehot(iota((R * 128, 128), 1) < 3)
    x = gate([nrm_ref[16 * i : 16 * i + 16] for i in range(R * 8)], marks, *SPAN[1])
    u = dot(jnp.concatenate([x, ones], 1), W1E[...])
    hid_ref[...] = (u * lax.erf(u) + u).astype(BF)


def kernel(
    fields, mask_in, CK, cb_in, gain_in, nb_in, W1, b1_in, W2, b2_in, ls_in, out,
    mask, cb, gain, nb, b1, b2, ls,
    NAT, XG0, XG1, CKV, KF, W1V, W1E, W2V, G4, H4, INS,
    acc, nrm, hid, EL, ER, LH, RH, FB, load_sem, send_sem, recv_sem, out_sem,
):
    lat, lon = lax.axis_index("lat"), lax.axis_index("lon")
    nlat, nlon = lax.axis_size("lat"), lax.axis_size("lon")
    right, left = lax.rem(lon + 1, nlon), lax.rem(lon + nlon - 1, nlon)
    fold = nlon - 1 - lon
    is_top, is_low = lat == nlat - 1, lat == 0
    not_top, not_low = lat < nlat - 1, lat > 0

    loads = [pltpu.make_async_copy(fields.at[pl.ds(12 * q, 12)], NAT.at[pl.ds(12 * q, 12)], load_sem.at[q]) for q in range(4)]
    loads += [
        pltpu.make_async_copy(CK, CKV, load_sem.at[4]),
        pltpu.make_async_copy(W1, W1V, load_sem.at[5]),
        pltpu.make_async_copy(W2, W2V, load_sem.at[6]),
        pltpu.make_async_copy(cb_in, cb, load_sem.at[7]),
        pltpu.make_async_copy(gain_in, gain, load_sem.at[8]),
        pltpu.make_async_copy(nb_in, nb, load_sem.at[9]),
        pltpu.make_async_copy(b1_in, b1, load_sem.at[10]),
        pltpu.make_async_copy(b2_in, b2, load_sem.at[11]),
        pltpu.make_async_copy(ls_in, ls, load_sem.at[12]),
    ]
    mask_load = pltpu.make_async_copy(mask_in, mask, load_sem.at[13])
    mask_load.start()
    for cp in loads:
        cp.start()

    barrier = pltpu.get_barrier_semaphore()

    def greet(a, o):
        pl.semaphore_signal(barrier, inc=1, device_id={"lat": a, "lon": o}, device_id_type=MESH)

    greet(lat, left)
    greet(lat, right)

    @pl.when(not_low)
    def _():
        greet(lat - 1, lon)

    @pl.when(not_top)
    def _():
        greet(lat + 1, lon)

    @pl.when(is_top)
    def _():
        greet(lat, fold)

    def remote(src, dst, i, j, a, o):
        return pltpu.make_async_remote_copy(
            src_ref=src, dst_ref=dst, send_sem=send_sem.at[i], recv_sem=recv_sem.at[j],
            device_id={"lat": a, "lon": o}, device_id_type=MESH,
        )

    n, c = iota((256, 128), 0), iota((256, 128), 1)
    col = 8 * (n % 16) + n // 16 - 3
    h, hc = iota((128, 128), 0), iota((128, 128), 1)
    for rr in range(R):
        en = n % 16 - 4 * rr
        okn = (en >= 0) & (en < 3)
        lsrc, rsrc = jnp.where(okn, en, -1), jnp.where(okn, 125 + en, -1)
        G4[rr] = onehot(jnp.where(n < 224, col, jnp.where(n < 240, lsrc, rsrc)) == c)
    f, fc = iota((160, 128), 0), iota((160, 128), 1)
    kk, g16 = f // 16, f % 16
    gsrc = jnp.where(kk < 3, g16 - 1, g16 + 1)
    hsrc = jnp.where((gsrc >= 0) & (gsrc < 16), jnp.where(kk < 3, kk + 5, kk - 3) * 16 + gsrc, -1)
    for p in range(R // 2):
        e = g16 - 4 * jnp.where(kk < 8, 2 * p, 2 * p + 1)
        src = jnp.where(kk % 2 == 0, e * 16, (5 + e) * 16 + 15)
        H4[p] = onehot(jnp.where(kk < 6, hsrc, jnp.where((e >= 0) & (e < 3), src, -1)) == fc)
    m, mc = iota((96 * R, 32), 0), iota((96 * R, 32), 1)
    mr, mk, mg = m // 96, (m % 96) // 16, m % 16
    INS[...] = onehot(jnp.where(mk < 3, jnp.where(mg == 0, 4 * mr + mk, -1), jnp.where(mg == 15, 13 + 4 * mr + mk, -1)) == mc)
    mask_load.wait()

    def pairs(b, lo, hi, base):
        a, z = 16 * lo, 16 * (hi - lo)
        return (
            remote(ER.at[b, pl.ds(a, z)], LH.at[b, pl.ds(a, z)], base, base, lat, right),
            remote(EL.at[b, pl.ds(a, z)], RH.at[b, pl.ds(a, z)], base + 1, base + 1, lat, left),
        )

    quarters = [pairs(0, 3 * q, 3 * q + 3, 2 * q) for q in range(4)]
    cols_a = pairs(1, 1, 5, 8)
    cols_b = pairs(1, 5, 8, 10)
    cols_c = pairs(1, 0, 1, 12) + pairs(1, 11, 12, 14)
    cols_d = pairs(1, 8, 9, 16)
    cols_e = pairs(1, 9, 11, 18)
    cols = [cp for p in quarters for cp in p] + [*cols_a, *cols_b, *cols_c, *cols_d, *cols_e]

    def rows(XG, b):
        i = 20 + 3 * b
        north = remote(XG.at[pl.ds(48, 3)], XG.at[pl.ds(0, 3)], i, i, lat + 1, lon)
        across = remote(XG.at[pl.ds(48, 3)], FB.at[b], i + 1, i + 1, lat, fold)
        south = remote(XG.at[pl.ds(3, 3)], XG.at[pl.ds(51, 3)], i + 2, i + 2, lat - 1, lon)
        return north, across, south

    rows0, rows1 = rows(XG0, 0), rows(XG1, 1)

    def send_rows(copies):
        north, across, south = copies
        pl.when(not_top)(north.start)
        pl.when(is_top)(across.start)
        pl.when(not_low)(south.start)

    def wait_rows(XG, b, copies):
        north, across, south = copies
        pl.when(not_low)(north.wait_recv)

        @pl.when(is_low)
        def _():
            XG[0:3] = jnp.zeros((3, 14, 16, 128), BF)

        pl.when(not_top)(south.wait_recv)

        @pl.when(is_top)
        def _():
            across.wait_recv()
            flip = onehot(iota((224, 224), 0) + iota((224, 224), 1) == 223)
            for j in range(3):
                XG[51 + j] = dot(flip, FB[b, 2 - j].reshape(224, 128)).astype(BF).reshape(14, 16, 128)

    def insert(XG, b, ch):
        at = pl.ds(pl.multiple_of(16 * ch, 16), 16)
        o = dot(INS[...], jnp.concatenate([LH[b, at], RH[b, at]], 0)).astype(BF)
        for rr in range(R):
            row = R * ch + rr + 3
            XG[row, 0:3] = XG[row, 0:3] + o[rr * 96 : rr * 96 + 48].reshape(3, 16, 128)
            XG[row, 11:14] = XG[row, 11:14] + o[rr * 96 + 48 : rr * 96 + 96].reshape(3, 16, 128)

    def edges(b, ch, el, er):
        at = pl.ds(pl.multiple_of(16 * ch, 16), 16)
        EL[b, at] = el.astype(BF)
        ER[b, at] = er.astype(BF)

    def prep(ch, carry):
        el = er = None
        for rr in range(R):
            row = R * ch + rr
            mrow = jnp.broadcast_to(mask[pl.ds(row, 1), :].astype(F), (16, 128)).astype(BF)
            lhs = (G4[rr].reshape(16, 16, 128) * mrow[None]).reshape(256, 128)
            o = dot(lhs, NAT[row])
            XG0[row + 3] = o[:224].astype(BF).reshape(14, 16, 128)
            el = o[224:240] if el is None else el + o[224:240]
            er = o[240:256] if er is None else er + o[240:256]
        edges(0, ch, el, er)
        return carry

    def landed(copies):
        for cp in copies:
            cp.wait_recv()

    def insert_all(XG, b, lo, hi):
        def one(ch, carry):
            insert(XG, b, ch)
            return carry

        lax.fori_loop(lo, hi, one, 0)

    for i, q in enumerate((0, 3, 1, 2)):
        loads[q].wait()
        lax.fori_loop(3 * q, 3 * q + 3, prep, 0)
        if i == 0:
            @pl.when(not_low)
            def _():
                pl.semaphore_wait(barrier, 4)

            @pl.when(is_low)
            def _():
                pl.semaphore_wait(barrier, 3)

        for cp in quarters[q]:
            cp.start()
    for cp in loads[4:]:
        cp.wait()
    for b in range(2):
        for t in range(49):
            KF[b, t] = jnp.broadcast_to(CKV[t, b : b + 1, :], (8, 128))
        W1E[b, :128] = W1V[b]
        bb = b1[b : b + 1] * HALF
        hi = bb.astype(BF).astype(F)
        lo = (bb - hi).astype(BF).astype(F)
        z = iota((128, 512), 0)
        W1E[b, 128:] = jnp.where(z == 0, hi, jnp.where(z == 1, lo, jnp.where(z == 2, bb - hi - lo, 0.0))).astype(BF)
    landed(quarters[0] + quarters[3])
    insert_all(XG0, 0, 0, 3)
    insert_all(XG0, 0, 9, 12)
    send_rows(rows0)

    def conv_stage(b, q, par):
        return conv((XG0, XG1)[b], KF.at[b], jnp.broadcast_to(cb[b : b + 1], (16, 128)), acc.at[par], R * chunk(b, q))

    def norm_stage(b, q, par, marks):
        norm(acc.at[par], nrm.at[par], gain[b : b + 1] * (HALF * 128**0.5), nb[b : b + 1] * HALF)

    def hidden_stage(b, q, par, marks):
        expand_hidden(nrm.at[par], hid.at[par], W1E.at[b], marks)

    def out_stage(b, q, par, marks):
        XG = (XG0, XG1)[b]
        ch = chunk(b, q)
        first = gate([hid[par, 16 * i : 16 * i + 16, :128] for i in range(R * 8)], marks, *SPAN[0])
        y = dot(jnp.concatenate([first, hid[par, :, 128:]], 1), W2V[b])
        y = (y + b2[b : b + 1] * (1 / HALF)) * (ls[b : b + 1] * HALF)
        xs = []
        for rr in range(R):
            row = R * ch + rr
            res = XG[row + 3, 3:11].reshape(128, 128).astype(F)
            x = (res + y[rr * 128 : rr * 128 + 128]).astype(BF)
            xs.append(x)
            if b == 0:
                XG1[row + 3, 3:11] = x.reshape(8, 16, 128)
            else:
                NAT[row] = x
        if b == 0:
            el = er = None
            for p in range(R // 2):
                o = dot(H4[p], jnp.concatenate(xs[2 * p : 2 * p + 2], 1))
                for i in range(2):
                    row = R * ch + 2 * p + i + 3
                    v = o[:, 128 * i : 128 * i + 128]
                    XG1[row, 0:3] = v[:48].astype(BF).reshape(3, 16, 128)
                    XG1[row, 11:14] = v[48:96].astype(BF).reshape(3, 16, 128)
                    a, z = v[96 + 32 * i : 112 + 32 * i], v[112 + 32 * i : 128 + 32 * i]
                    el, er = (a, z) if el is None else (el + a, er + z)
            edges(1, ch, el, er)

    def finish(ch):
        return pltpu.make_async_copy(NAT.at[pl.ds(R * ch, R)], out.at[pl.ds(R * ch, R)], out_sem.at[ch])

    stages = (out_stage, hidden_stage, norm_stage)

    def step(b, q, par):
        marks = conv_stage(b, q + 3, (par + 3) % 2)
        for d, stage in enumerate(stages):
            stage(b, q + d, (par + d) % 2, marks)

    def mixed(s):
        i = s + 3
        marks = conv_stage(i // N, i % N, i % 2) if i < 2 * N else []
        for d, stage in enumerate(stages):
            i = s + d
            if 0 <= i < 2 * N:
                stage(i // N, i % N, i % 2, marks)

    mixed(-3)
    landed(quarters[1] + quarters[2])
    insert_all(XG0, 0, 3, 9)
    mixed(-2)
    mixed(-1)

    def body0(j, carry):
        @pl.when(j == 2)
        def _():
            wait_rows(XG0, 0, rows0)
            for cp in cols_a:
                cp.start()

        step(0, 2 * j, 0)
        step(0, 2 * j + 1, 1)
        return carry

    lax.fori_loop(0, 4, body0, 0)
    for cp in cols_b:
        cp.start()
    mixed(8)
    for cp in cols_c:
        cp.start()
    landed(cols_a)
    insert_all(XG1, 1, 1, 5)
    mixed(9)
    for cp in cols_d:
        cp.start()
    mixed(10)
    landed(cols_b)
    insert_all(XG1, 1, 5, 8)
    mixed(11)
    for cp in cols_e:
        cp.start()
    landed(cols_c)
    insert(XG1, 1, 0)
    insert(XG1, 1, 11)
    send_rows(rows1)

    def body1(j, carry):
        @pl.when(j == 1)
        def _():
            landed(cols_d)
            insert(XG1, 1, 8)

        @pl.when(j == 2)
        def _():
            landed(cols_e)
            insert_all(XG1, 1, 9, 11)

        @pl.when(j == 3)
        def _():
            wait_rows(XG1, 1, rows1)

        step(1, 2 * j, 0)
        step(1, 2 * j + 1, 1)
        finish(chunk(1, 2 * j)).start()
        finish(chunk(1, 2 * j + 1)).start()
        return carry

    lax.fori_loop(0, 4, body1, 0)
    for s in range(20, 24):
        mixed(s)
        finish(chunk(1, s - N)).start()
    for cp in cols:
        cp.wait_send()
    for north, across, south in (rows0, rows1):
        pl.when(not_top)(north.wait_send)
        pl.when(is_top)(across.wait_send)
        pl.when(not_low)(south.wait_send)
    for ch in range(N):
        finish(ch).wait()


def ungroup(x, mask, out, xv, ov, mv, sem_in, sem_out):
    def fetch(q):
        return pltpu.make_async_copy(x.at[pl.ds(q * TAIL, TAIL)], xv.at[pl.ds(q * TAIL, TAIL)], sem_in.at[q])

    def put(q):
        return pltpu.make_async_copy(ov.at[pl.ds(q * TAIL, TAIL)], out.at[pl.ds(q * TAIL, TAIL)], sem_out.at[q])

    steps = ROWS // TAIL
    mask_load = pltpu.make_async_copy(mask, mv, sem_in.at[steps])
    mask_load.start()
    for q in range(steps):
        fetch(q).start()
    h, hc = iota((128, 128), 0), iota((128, 128), 1)
    order = onehot((h % 8) * 16 + h // 8 == hc)
    mask_load.wait()
    wet = jnp.transpose(mv[...].astype(F))
    for q in range(steps):
        fetch(q).wait()
        for p in range(q * TAIL, q * TAIL + TAIL, 2):
            o = dot(order, jnp.concatenate([xv[p], xv[p + 1]], 1))
            for i in range(2):
                ov[p + i] = (o[:, 128 * i : 128 * i + 128] * wet[:, p + i : p + i + 1]).astype(BF)
        put(q).start()
    for q in range(steps):
        put(q).wait()


def shards(fields, wet_mask, *w):
    CK, cb, gain, nb, W1, b1, W2, b2, ls = w
    V = pltpu.VMEM
    grouped = pl.pallas_call(
        kernel,
        out_shape=jax.ShapeDtypeStruct((ROWS, COLS, C), BF),
        in_specs=[pl.BlockSpec(memory_space=pltpu.HBM)] * 11,
        out_specs=pl.BlockSpec(memory_space=pl.ANY),
        scratch_shapes=[
            V((ROWS, COLS), jnp.int32), V((2, C), F), V((2, C), F), V((2, C), F), V((2, 512), F), V((2, C), F), V((2, C), F),
            V((ROWS, COLS, C), BF), V((54, 14, 16, C), BF), V((54, 14, 16, C), BF),
            V((49, 2, C), F), V((2, 49, 8, C), F), V((2, 128, 512), BF), V((2, 256, 512), BF), V((2, 512, 128), BF),
            V((R, 256, 128), BF), V((R // 2, 160, 128), BF), V((96 * R, 32), BF),
            V((2, R * 128, C), F), V((2, R * 128, C), BF), V((2, R * 128, 512), BF),
            V((2, 192, C), BF), V((2, 192, C), BF), V((2, 192, C), BF), V((2, 192, C), BF), V((2, 3, 14, 16, C), BF),
            pltpu.SemaphoreType.DMA((14,)), pltpu.SemaphoreType.DMA((26,)), pltpu.SemaphoreType.DMA((26,)), pltpu.SemaphoreType.DMA((N,)),
        ],
        compiler_params=pltpu.CompilerParams(vmem_limit_bytes=VMB << 20, collective_id=0, has_side_effects=True),
        name="forecast",
    )(fields, wet_mask, jnp.transpose(CK, (1, 0, 2)), *w[1:])
    return pl.pallas_call(
        ungroup,
        out_shape=jax.ShapeDtypeStruct((ROWS, COLS, C), BF),
        in_specs=[pl.BlockSpec(memory_space=pl.ANY)] * 2,
        out_specs=pl.BlockSpec(memory_space=pl.ANY),
        scratch_shapes=[
            V((ROWS, COLS, C), BF), V((ROWS, COLS, C), BF), V((ROWS, COLS), jnp.int32),
            pltpu.SemaphoreType.DMA((ROWS // TAIL + 1,)), pltpu.SemaphoreType.DMA((ROWS // TAIL,)),
        ],
        compiler_params=pltpu.CompilerParams(vmem_limit_bytes=VMB << 20),
        name="ungroup",
    )(grouped, wet_mask)


def solution(mesh):
    return jax.shard_map(
        shards, mesh=mesh, in_specs=(P("lat", "lon", None), P("lat", "lon")) + (P(),) * 9,
        out_specs=P("lat", "lon", None), check_vma=False,
    )
```

```python
import functools

import jax
import jax.numpy as jnp
from jax import lax
from jax.experimental import pallas as pl
from jax.experimental.pallas import tpu as pltpu
from jax.sharding import PartitionSpec as P

BF, F = jnp.bfloat16, jnp.float32
R = 4
ROWS, COLS, C = 48, 128, 128
N = ROWS // R
MESH = pl.DeviceIdType.MESH
VMB = 60
TAIL = 8
HALF = 0.7071067811865476
SPAN = ((0, 14), (14, 28))


def iota(shape, d):
    return lax.broadcasted_iota(jnp.int32, shape, d)


def onehot(cond):
    return jnp.where(cond, 1.0, 0.0).astype(BF)


def dot(a, b):
    return jnp.dot(a, b, preferred_element_type=F)


def tree(v):
    while len(v) > 1:
        v = [v[i] + v[i + 1] if i + 1 < len(v) else v[i] for i in range(0, len(v), 2)]
    return v[0]


ORDER = ([1, 2, 3, 4, 5, 6, 7, 0, 11, 8, 9, 10], [2, 3, 4, 5, 6, 1, 7, 8, 9, 10, 0, 11])


def chunk(b, q):
    if isinstance(q, int):
        return ORDER[b][q]
    if b == 0:
        return jnp.where(q < 7, q + 1, jnp.where(q == 7, 0, jnp.where(q == 8, 11, q - 1)))
    return jnp.where(q < 5, q + 2, jnp.where(q == 5, 1, jnp.where(q < 10, q + 1, (q - 10) * 11)))


def gate(pieces, marks, lo, hi):
    if not marks:
        return jnp.concatenate(pieces, 0)
    n = len(pieces)
    return jnp.concatenate([p + marks[lo + i * (hi - lo) // n] for i, p in enumerate(pieces)], 0)


def conv(XG, KF, bias, acc_ref, row0):
    marks = []
    for rr in range(R):
        acc = [bias] * 8
        for r in range(7):
            xs = [XG[row0 + rr + r, k] for k in range(14)]
            ws = []
            for s in range(7):
                w = KF[7 * r + s]
                ws.append(jnp.concatenate([w, w], 0).astype(BF))
            for k in range(8):
                part = tree([ws[s] * xs[k + s] for s in range(7)])
                acc[k] = acc[k] + part.astype(F)
            marks.append(part * BF(0))
        for k in range(8):
            acc_ref[rr * 128 + k * 16 : rr * 128 + k * 16 + 16, :] = acc[k]
    return marks


def norm(acc_ref, out_ref, gain, nb):
    c = acc_ref[...]
    cen = c - jnp.sum(c, axis=-1, keepdims=True) * (1 / 128)
    var = jnp.sum(cen * cen, axis=-1, keepdims=True)
    out_ref[...] = (cen * lax.rsqrt(var + 128e-6) * gain + nb).astype(BF)


def expand_hidden(nrm_ref, hid_ref, W1E, marks):
    ones = onehot(iota((R * 128, 128), 1) < 3)
    x = gate([nrm_ref[16 * i : 16 * i + 16] for i in range(R * 8)], marks, *SPAN[1])
    u = dot(jnp.concatenate([x, ones], 1), W1E[...])
    hid_ref[...] = (u * lax.erf(u) + u).astype(BF)


def kernel(
    fields, mask_in, CK, cb_in, gain_in, nb_in, W1, b1_in, W2, b2_in, ls_in, out,
    mask, cb, gain, nb, b1, b2, ls,
    NAT, XG0, XG1, CKV, KF, W1V, W1E, W2V, G4, H4, INS,
    acc, nrm, hid, EL, ER, LH, RH, FB, load_sem, send_sem, recv_sem, out_sem,
):
    lat, lon = lax.axis_index("lat"), lax.axis_index("lon")
    nlat, nlon = lax.axis_size("lat"), lax.axis_size("lon")
    right, left = lax.rem(lon + 1, nlon), lax.rem(lon + nlon - 1, nlon)
    fold = nlon - 1 - lon
    is_top, is_low = lat == nlat - 1, lat == 0
    not_top, not_low = lat < nlat - 1, lat > 0

    loads = [pltpu.make_async_copy(fields.at[pl.ds(12 * q, 12)], NAT.at[pl.ds(12 * q, 12)], load_sem.at[q]) for q in range(4)]
    loads += [
        pltpu.make_async_copy(CK, CKV, load_sem.at[4]),
        pltpu.make_async_copy(W1, W1V, load_sem.at[5]),
        pltpu.make_async_copy(W2, W2V, load_sem.at[6]),
        pltpu.make_async_copy(cb_in, cb, load_sem.at[7]),
        pltpu.make_async_copy(gain_in, gain, load_sem.at[8]),
        pltpu.make_async_copy(nb_in, nb, load_sem.at[9]),
        pltpu.make_async_copy(b1_in, b1, load_sem.at[10]),
        pltpu.make_async_copy(b2_in, b2, load_sem.at[11]),
        pltpu.make_async_copy(ls_in, ls, load_sem.at[12]),
    ]
    mask_load = pltpu.make_async_copy(mask_in, mask, load_sem.at[13])
    mask_load.start()
    for cp in loads:
        cp.start()

    barrier = pltpu.get_barrier_semaphore()

    def greet(a, o):
        pl.semaphore_signal(barrier, inc=1, device_id={"lat": a, "lon": o}, device_id_type=MESH)

    greet(lat, left)
    greet(lat, right)

    @pl.when(not_low)
    def _():
        greet(lat - 1, lon)

    @pl.when(not_top)
    def _():
        greet(lat + 1, lon)

    @pl.when(is_top)
    def _():
        greet(lat, fold)

    def remote(src, dst, i, j, a, o):
        return pltpu.make_async_remote_copy(
            src_ref=src, dst_ref=dst, send_sem=send_sem.at[i], recv_sem=recv_sem.at[j],
            device_id={"lat": a, "lon": o}, device_id_type=MESH,
        )

    n, c = iota((288, 128), 0), iota((288, 128), 1)
    col = 8 * (n % 16) + n // 16 - 3
    for p in range(R // 2):
        en = n % 16 - 4 * jnp.where(n < 256, 2 * p, 2 * p + 1)
        src = jnp.where((n // 16) % 2 == 0, en, 125 + en)
        G4[p] = onehot(jnp.where(n < 224, col, jnp.where((en >= 0) & (en < 3), src, -1)) == c)
    f, fc = iota((160, 128), 0), iota((160, 128), 1)
    kk, g16 = f // 16, f % 16
    gsrc = jnp.where(kk < 3, g16 - 1, g16 + 1)
    hsrc = jnp.where((gsrc >= 0) & (gsrc < 16), jnp.where(kk < 3, kk + 5, kk - 3) * 16 + gsrc, -1)
    for p in range(R // 2):
        e = g16 - 4 * jnp.where(kk < 8, 2 * p, 2 * p + 1)
        src = jnp.where(kk % 2 == 0, e * 16, (5 + e) * 16 + 15)
        H4[p] = onehot(jnp.where(kk < 6, hsrc, jnp.where((e >= 0) & (e < 3), src, -1)) == fc)
    m, mc = iota((96 * R, 32), 0), iota((96 * R, 32), 1)
    mr, mk, mg = m // 96, (m % 96) // 16, m % 16
    INS[...] = onehot(jnp.where(mk < 3, jnp.where(mg == 0, 4 * mr + mk, -1), jnp.where(mg == 15, 13 + 4 * mr + mk, -1)) == mc)
    mask_load.wait()

    def pairs(b, lo, hi, base):
        a, z = 16 * lo, 16 * (hi - lo)
        return (
            remote(ER.at[b, pl.ds(a, z)], LH.at[b, pl.ds(a, z)], base, base, lat, right),
            remote(EL.at[b, pl.ds(a, z)], RH.at[b, pl.ds(a, z)], base + 1, base + 1, lat, left),
        )

    quarters = [pairs(0, 3 * q, 3 * q + 3, 2 * q) for q in range(4)]
    cols_a = pairs(1, 1, 5, 8)
    cols_b = pairs(1, 5, 8, 10)
    cols_c = pairs(1, 0, 1, 12) + pairs(1, 11, 12, 14)
    cols_d = pairs(1, 8, 9, 16)
    cols_e = pairs(1, 9, 11, 18)
    cols = [cp for p in quarters for cp in p] + [*cols_a, *cols_b, *cols_c, *cols_d, *cols_e]

    def rows(XG, b):
        i = 20 + 3 * b
        north = remote(XG.at[pl.ds(48, 3)], XG.at[pl.ds(0, 3)], i, i, lat + 1, lon)
        across = remote(XG.at[pl.ds(48, 3)], FB.at[b], i + 1, i + 1, lat, fold)
        south = remote(XG.at[pl.ds(3, 3)], XG.at[pl.ds(51, 3)], i + 2, i + 2, lat - 1, lon)
        return north, across, south

    rows0, rows1 = rows(XG0, 0), rows(XG1, 1)

    def send_rows(copies):
        north, across, south = copies
        pl.when(not_top)(north.start)
        pl.when(is_top)(across.start)
        pl.when(not_low)(south.start)

    def wait_rows(XG, b, copies):
        north, across, south = copies
        pl.when(not_low)(north.wait_recv)

        @pl.when(is_low)
        def _():
            XG[0:3] = jnp.zeros((3, 14, 16, 128), BF)

        pl.when(not_top)(south.wait_recv)

        @pl.when(is_top)
        def _():
            across.wait_recv()
            flip = onehot(iota((224, 224), 0) + iota((224, 224), 1) == 223)
            for j in range(3):
                XG[51 + j] = dot(flip, FB[b, 2 - j].reshape(224, 128)).astype(BF).reshape(14, 16, 128)

    def insert(XG, b, ch):
        at = pl.ds(pl.multiple_of(16 * ch, 16), 16)
        o = dot(INS[...], jnp.concatenate([LH[b, at], RH[b, at]], 0)).astype(BF)
        for rr in range(R):
            row = R * ch + rr + 3
            XG[row, 0:3] = XG[row, 0:3] + o[rr * 96 : rr * 96 + 48].reshape(3, 16, 128)
            XG[row, 11:14] = XG[row, 11:14] + o[rr * 96 + 48 : rr * 96 + 96].reshape(3, 16, 128)

    def edges(b, ch, el, er):
        at = pl.ds(16 * ch if isinstance(ch, int) else pl.multiple_of(16 * ch, 16), 16)
        EL[b, at] = el.astype(BF)
        ER[b, at] = er.astype(BF)

    wet = jnp.transpose(mask[...].astype(F))

    def prep(ch):
        el = er = None
        for p in range(R // 2):
            row = R * ch + 2 * p
            both = [NAT[row + i] * jnp.broadcast_to(wet[:, row + i : row + i + 1], (COLS, C)).astype(BF) for i in range(2)]
            o = dot(G4[p], jnp.concatenate(both, 1))
            for i in range(2):
                v = o[:, C * i : C * i + C]
                XG0[row + i + 3] = v[:224].astype(BF).reshape(14, 16, 128)
                a, z = v[224 + 32 * i : 240 + 32 * i], v[240 + 32 * i : 256 + 32 * i]
                el, er = (a, z) if el is None else (el + a, er + z)
        edges(0, ch, el, er)

    def landed(copies):
        for cp in copies:
            cp.wait_recv()

    def insert_all(XG, b, lo, hi):
        def one(ch, carry):
            insert(XG, b, ch)
            return carry

        lax.fori_loop(lo, hi, one, 0)

    for i, q in enumerate((0, 3, 1, 2)):
        loads[q].wait()
        for ch in range(3 * q, 3 * q + 3):
            prep(ch)
        if i == 0:
            @pl.when(not_low)
            def _():
                pl.semaphore_wait(barrier, 4)

            @pl.when(is_low)
            def _():
                pl.semaphore_wait(barrier, 3)

        for cp in quarters[q]:
            cp.start()
    for cp in loads[4:]:
        cp.wait()
    for b in range(2):
        for t in range(49):
            KF[b, t] = jnp.broadcast_to(CKV[t, b : b + 1, :], (8, 128))
        W1E[b, :128] = W1V[b]
        bb = b1[b : b + 1] * HALF
        hi = bb.astype(BF).astype(F)
        lo = (bb - hi).astype(BF).astype(F)
        z = iota((128, 512), 0)
        W1E[b, 128:] = jnp.where(z == 0, hi, jnp.where(z == 1, lo, jnp.where(z == 2, bb - hi - lo, 0.0))).astype(BF)
    landed(quarters[0] + quarters[3])
    insert_all(XG0, 0, 0, 3)
    insert_all(XG0, 0, 9, 12)
    send_rows(rows0)

    def conv_stage(b, q, par):
        return conv((XG0, XG1)[b], KF.at[b], jnp.broadcast_to(cb[b : b + 1], (16, 128)), acc.at[par], R * chunk(b, q))

    def norm_stage(b, q, par, marks):
        norm(acc.at[par], nrm.at[par], gain[b : b + 1] * (HALF * 128**0.5), nb[b : b + 1] * HALF)

    def hidden_stage(b, q, par, marks):
        expand_hidden(nrm.at[par], hid.at[par], W1E.at[b], marks)

    def out_stage(b, q, par, marks):
        XG = (XG0, XG1)[b]
        ch = chunk(b, q)
        first = gate([hid[par, 16 * i : 16 * i + 16, :128] for i in range(R * 8)], marks, *SPAN[0])
        y = dot(jnp.concatenate([first, hid[par, :, 128:]], 1), W2V[b])
        y = (y + b2[b : b + 1] * (1 / HALF)) * (ls[b : b + 1] * HALF)
        xs = []
        for rr in range(R):
            row = R * ch + rr
            res = XG[row + 3, 3:11].reshape(128, 128).astype(F)
            x = (res + y[rr * 128 : rr * 128 + 128]).astype(BF)
            xs.append(x)
            if b == 0:
                XG1[row + 3, 3:11] = x.reshape(8, 16, 128)
            else:
                NAT[row] = x
        if b == 0:
            el = er = None
            for p in range(R // 2):
                o = dot(H4[p], jnp.concatenate(xs[2 * p : 2 * p + 2], 1))
                for i in range(2):
                    row = R * ch + 2 * p + i + 3
                    v = o[:, 128 * i : 128 * i + 128]
                    XG1[row, 0:3] = v[:48].astype(BF).reshape(3, 16, 128)
                    XG1[row, 11:14] = v[48:96].astype(BF).reshape(3, 16, 128)
                    a, z = v[96 + 32 * i : 112 + 32 * i], v[112 + 32 * i : 128 + 32 * i]
                    el, er = (a, z) if el is None else (el + a, er + z)
            edges(1, ch, el, er)

    def finish(ch):
        return pltpu.make_async_copy(NAT.at[pl.ds(R * ch, R)], out.at[pl.ds(R * ch, R)], out_sem.at[ch])

    stages = (out_stage, hidden_stage, norm_stage)

    def step(b, q, par):
        marks = conv_stage(b, q + 3, (par + 3) % 2)
        for d, stage in enumerate(stages):
            stage(b, q + d, (par + d) % 2, marks)

    def mixed(s):
        i = s + 3
        marks = conv_stage(i // N, i % N, i % 2) if i < 2 * N else []
        for d, stage in enumerate(stages):
            i = s + d
            if 0 <= i < 2 * N:
                stage(i // N, i % N, i % 2, marks)

    mixed(-3)
    landed(quarters[1] + quarters[2])
    insert_all(XG0, 0, 3, 9)
    mixed(-2)
    mixed(-1)

    def body0(j, carry):
        @pl.when(j == 2)
        def _():
            wait_rows(XG0, 0, rows0)
            for cp in cols_a:
                cp.start()

        step(0, 2 * j, 0)
        step(0, 2 * j + 1, 1)
        return carry

    lax.fori_loop(0, 4, body0, 0)
    for cp in cols_b:
        cp.start()
    mixed(8)
    for cp in cols_c:
        cp.start()
    landed(cols_a)
    insert_all(XG1, 1, 1, 5)
    mixed(9)
    for cp in cols_d:
        cp.start()
    mixed(10)
    landed(cols_b)
    insert_all(XG1, 1, 5, 8)
    mixed(11)
    for cp in cols_e:
        cp.start()
    landed(cols_c)
    insert(XG1, 1, 0)
    insert(XG1, 1, 11)
    send_rows(rows1)

    def body1(j, carry):
        @pl.when(j == 1)
        def _():
            landed(cols_d)
            insert(XG1, 1, 8)

        @pl.when(j == 2)
        def _():
            landed(cols_e)
            insert_all(XG1, 1, 9, 11)

        @pl.when(j == 3)
        def _():
            wait_rows(XG1, 1, rows1)

        step(1, 2 * j, 0)
        step(1, 2 * j + 1, 1)
        finish(chunk(1, 2 * j)).start()
        finish(chunk(1, 2 * j + 1)).start()
        return carry

    lax.fori_loop(0, 4, body1, 0)
    for s in range(20, 24):
        mixed(s)
        finish(chunk(1, s - N)).start()
    for cp in cols:
        cp.wait_send()
    for north, across, south in (rows0, rows1):
        pl.when(not_top)(north.wait_send)
        pl.when(is_top)(across.wait_send)
        pl.when(not_low)(south.wait_send)
    for ch in range(N):
        finish(ch).wait()


def ungroup(x, mask, out, xv, ov, mv, sem_in, sem_out):
    def fetch(q):
        return pltpu.make_async_copy(x.at[pl.ds(q * TAIL, TAIL)], xv.at[pl.ds(q * TAIL, TAIL)], sem_in.at[q])

    def put(q):
        return pltpu.make_async_copy(ov.at[pl.ds(q * TAIL, TAIL)], out.at[pl.ds(q * TAIL, TAIL)], sem_out.at[q])

    steps = ROWS // TAIL
    mask_load = pltpu.make_async_copy(mask, mv, sem_in.at[steps])
    mask_load.start()
    for q in range(steps):
        fetch(q).start()
    h, hc = iota((128, 128), 0), iota((128, 128), 1)
    order = onehot((h % 8) * 16 + h // 8 == hc)
    mask_load.wait()
    wet = jnp.transpose(mv[...].astype(F))
    for q in range(steps):
        fetch(q).wait()
        for p in range(q * TAIL, q * TAIL + TAIL, 2):
            o = dot(order, jnp.concatenate([xv[p], xv[p + 1]], 1))
            for i in range(2):
                ov[p + i] = (o[:, 128 * i : 128 * i + 128] * wet[:, p + i : p + i + 1]).astype(BF)
        put(q).start()
    for q in range(steps):
        put(q).wait()


def shards(fields, wet_mask, *w):
    CK, cb, gain, nb, W1, b1, W2, b2, ls = w
    V = pltpu.VMEM
    grouped = pl.pallas_call(
        kernel,
        out_shape=jax.ShapeDtypeStruct((ROWS, COLS, C), BF),
        in_specs=[pl.BlockSpec(memory_space=pltpu.HBM)] * 11,
        out_specs=pl.BlockSpec(memory_space=pl.ANY),
        scratch_shapes=[
            V((ROWS, COLS), jnp.int32), V((2, C), F), V((2, C), F), V((2, C), F), V((2, 512), F), V((2, C), F), V((2, C), F),
            V((ROWS, COLS, C), BF), V((54, 14, 16, C), BF), V((54, 14, 16, C), BF),
            V((49, 2, C), F), V((2, 49, 8, C), F), V((2, 128, 512), BF), V((2, 256, 512), BF), V((2, 512, 128), BF),
            V((R // 2, 288, 128), BF), V((R // 2, 160, 128), BF), V((96 * R, 32), BF),
            V((2, R * 128, C), F), V((2, R * 128, C), BF), V((2, R * 128, 512), BF),
            V((2, 192, C), BF), V((2, 192, C), BF), V((2, 192, C), BF), V((2, 192, C), BF), V((2, 3, 14, 16, C), BF),
            pltpu.SemaphoreType.DMA((14,)), pltpu.SemaphoreType.DMA((26,)), pltpu.SemaphoreType.DMA((26,)), pltpu.SemaphoreType.DMA((N,)),
        ],
        compiler_params=pltpu.CompilerParams(vmem_limit_bytes=VMB << 20, collective_id=0, has_side_effects=True),
        name="forecast",
    )(fields, wet_mask, jnp.transpose(CK, (1, 0, 2)), *w[1:])
    return pl.pallas_call(
        ungroup,
        out_shape=jax.ShapeDtypeStruct((ROWS, COLS, C), BF),
        in_specs=[pl.BlockSpec(memory_space=pl.ANY)] * 2,
        out_specs=pl.BlockSpec(memory_space=pl.ANY),
        scratch_shapes=[
            V((ROWS, COLS, C), BF), V((ROWS, COLS, C), BF), V((ROWS, COLS), jnp.int32),
            pltpu.SemaphoreType.DMA((ROWS // TAIL + 1,)), pltpu.SemaphoreType.DMA((ROWS // TAIL,)),
        ],
        compiler_params=pltpu.CompilerParams(vmem_limit_bytes=VMB << 20),
        name="ungroup",
    )(grouped, wet_mask)


def solution(mesh):
    return jax.shard_map(
        shards, mesh=mesh, in_specs=(P("lat", "lon", None), P("lat", "lon")) + (P(),) * 9,
        out_specs=P("lat", "lon", None), check_vma=False,
    )
```

```python
import functools

import jax
import jax.numpy as jnp
from jax import lax
from jax.experimental import pallas as pl
from jax.experimental.pallas import tpu as pltpu
from jax.sharding import PartitionSpec as P

BF, F = jnp.bfloat16, jnp.float32
R = 4
ROWS, COLS, C = 48, 128, 128
N = ROWS // R
MESH = pl.DeviceIdType.MESH
VMB = 60
TAIL = 12
HALF = 0.7071067811865476
SPAN = ((0, 14), (14, 28))


def iota(shape, d):
    return lax.broadcasted_iota(jnp.int32, shape, d)


def onehot(cond):
    return jnp.where(cond, 1.0, 0.0).astype(BF)


def dot(a, b):
    return jnp.dot(a, b, preferred_element_type=F)


def tree(v):
    while len(v) > 1:
        v = [v[i] + v[i + 1] if i + 1 < len(v) else v[i] for i in range(0, len(v), 2)]
    return v[0]


ORDER = ([1, 2, 3, 4, 5, 6, 7, 0, 11, 8, 9, 10], [2, 3, 4, 5, 6, 1, 7, 8, 9, 10, 0, 11])


def chunk(b, q):
    if isinstance(q, int):
        return ORDER[b][q]
    if b == 0:
        return jnp.where(q < 7, q + 1, jnp.where(q == 7, 0, jnp.where(q == 8, 11, q - 1)))
    return jnp.where(q < 5, q + 2, jnp.where(q == 5, 1, jnp.where(q < 10, q + 1, (q - 10) * 11)))


def gate(pieces, marks, lo, hi):
    if not marks:
        return jnp.concatenate(pieces, 0)
    n = len(pieces)
    return jnp.concatenate([p + marks[lo + i * (hi - lo) // n] for i, p in enumerate(pieces)], 0)


def conv(XG, KF, bias, acc_ref, row0):
    marks = []
    for rr in range(R):
        acc = [bias] * 8
        for r in range(7):
            xs = [XG[row0 + rr + r, k] for k in range(14)]
            ws = []
            for s in range(7):
                w = KF[7 * r + s]
                ws.append(jnp.concatenate([w, w], 0).astype(BF))
            for k in range(8):
                part = tree([ws[s] * xs[k + s] for s in range(7)])
                acc[k] = acc[k] + part.astype(F)
            marks.append(part * BF(0))
        for k in range(8):
            acc_ref[rr * 128 + k * 16 : rr * 128 + k * 16 + 16, :] = acc[k]
    return marks


def norm(acc_ref, out_ref, gain, nb):
    c = acc_ref[...]
    cen = c - jnp.sum(c, axis=-1, keepdims=True) * (1 / 128)
    var = jnp.sum(cen * cen, axis=-1, keepdims=True)
    out_ref[...] = (cen * lax.rsqrt(var + 128e-6) * gain + nb).astype(BF)


def expand_hidden(nrm_ref, hid_ref, W1E, marks):
    ones = onehot(iota((R * 128, 128), 1) < 3)
    x = gate([nrm_ref[16 * i : 16 * i + 16] for i in range(R * 8)], marks, *SPAN[1])
    u = dot(jnp.concatenate([x, ones], 1), W1E[...])
    hid_ref[...] = (u * lax.erf(u) + u).astype(BF)


def kernel(
    fields, mask_in, CK, cb_in, gain_in, nb_in, W1, b1_in, W2, b2_in, ls_in, out,
    mask, cb, gain, nb, b1, b2, ls,
    NAT, XG0, XG1, CKV, KF, W1V, W1E, W2V, G4, H4, INS,
    acc, nrm, hid, EL, ER, LH, RH, FB, load_sem, send_sem, recv_sem, out_sem,
):
    lat, lon = lax.axis_index("lat"), lax.axis_index("lon")
    nlat, nlon = lax.axis_size("lat"), lax.axis_size("lon")
    right, left = lax.rem(lon + 1, nlon), lax.rem(lon + nlon - 1, nlon)
    fold = nlon - 1 - lon
    is_top, is_low = lat == nlat - 1, lat == 0
    not_top, not_low = lat < nlat - 1, lat > 0

    loads = [pltpu.make_async_copy(fields.at[pl.ds(12 * q, 12)], NAT.at[pl.ds(12 * q, 12)], load_sem.at[q]) for q in range(4)]
    loads += [
        pltpu.make_async_copy(CK, CKV, load_sem.at[4]),
        pltpu.make_async_copy(W1, W1V, load_sem.at[5]),
        pltpu.make_async_copy(W2, W2V, load_sem.at[6]),
        pltpu.make_async_copy(cb_in, cb, load_sem.at[7]),
        pltpu.make_async_copy(gain_in, gain, load_sem.at[8]),
        pltpu.make_async_copy(nb_in, nb, load_sem.at[9]),
        pltpu.make_async_copy(b1_in, b1, load_sem.at[10]),
        pltpu.make_async_copy(b2_in, b2, load_sem.at[11]),
        pltpu.make_async_copy(ls_in, ls, load_sem.at[12]),
    ]
    mask_load = pltpu.make_async_copy(mask_in, mask, load_sem.at[13])
    mask_load.start()
    for i in (0, 3, 1, 2, *range(4, len(loads))):
        loads[i].start()

    barrier = pltpu.get_barrier_semaphore()

    def greet(a, o):
        pl.semaphore_signal(barrier, inc=1, device_id={"lat": a, "lon": o}, device_id_type=MESH)

    greet(lat, left)
    greet(lat, right)

    @pl.when(not_low)
    def _():
        greet(lat - 1, lon)

    @pl.when(not_top)
    def _():
        greet(lat + 1, lon)

    @pl.when(is_top)
    def _():
        greet(lat, fold)

    def remote(src, dst, i, j, a, o):
        return pltpu.make_async_remote_copy(
            src_ref=src, dst_ref=dst, send_sem=send_sem.at[i], recv_sem=recv_sem.at[j],
            device_id={"lat": a, "lon": o}, device_id_type=MESH,
        )

    n, c = iota((288, 128), 0), iota((288, 128), 1)
    col = 8 * (n % 16) + n // 16 - 3
    for p in range(R // 2):
        en = n % 16 - 4 * jnp.where(n < 256, 2 * p, 2 * p + 1)
        src = jnp.where((n // 16) % 2 == 0, en, 125 + en)
        G4[p] = onehot(jnp.where(n < 224, col, jnp.where((en >= 0) & (en < 3), src, -1)) == c)
    f, fc = iota((160, 128), 0), iota((160, 128), 1)
    kk, g16 = f // 16, f % 16
    gsrc = jnp.where(kk < 3, g16 - 1, g16 + 1)
    hsrc = jnp.where((gsrc >= 0) & (gsrc < 16), jnp.where(kk < 3, kk + 5, kk - 3) * 16 + gsrc, -1)
    for p in range(R // 2):
        e = g16 - 4 * jnp.where(kk < 8, 2 * p, 2 * p + 1)
        src = jnp.where(kk % 2 == 0, e * 16, (5 + e) * 16 + 15)
        H4[p] = onehot(jnp.where(kk < 6, hsrc, jnp.where((e >= 0) & (e < 3), src, -1)) == fc)
    m, mc = iota((96 * R, 32), 0), iota((96 * R, 32), 1)
    mr, mk, mg = m // 96, (m % 96) // 16, m % 16
    INS[...] = onehot(jnp.where(mk < 3, jnp.where(mg == 0, 4 * mr + mk, -1), jnp.where(mg == 15, 13 + 4 * mr + mk, -1)) == mc)
    mask_load.wait()

    def pairs(b, lo, hi, base):
        a, z = 16 * lo, 16 * (hi - lo)
        return (
            remote(ER.at[b, pl.ds(a, z)], LH.at[b, pl.ds(a, z)], base, base, lat, right),
            remote(EL.at[b, pl.ds(a, z)], RH.at[b, pl.ds(a, z)], base + 1, base + 1, lat, left),
        )

    quarters = [pairs(0, 3 * q, 3 * q + 3, 2 * q) for q in range(4)]
    cols_a = pairs(1, 1, 5, 8)
    cols_b = pairs(1, 5, 8, 10)
    cols_c = pairs(1, 0, 1, 12) + pairs(1, 11, 12, 14)
    cols_d = pairs(1, 8, 9, 16)
    cols_e = pairs(1, 9, 11, 18)
    cols = [cp for p in quarters for cp in p] + [*cols_a, *cols_b, *cols_c, *cols_d, *cols_e]

    def rows(XG, b):
        i = 20 + 3 * b
        north = remote(XG.at[pl.ds(48, 3)], XG.at[pl.ds(0, 3)], i, i, lat + 1, lon)
        across = remote(XG.at[pl.ds(48, 3)], FB.at[b], i + 1, i + 1, lat, fold)
        south = remote(XG.at[pl.ds(3, 3)], XG.at[pl.ds(51, 3)], i + 2, i + 2, lat - 1, lon)
        return north, across, south

    rows0, rows1 = rows(XG0, 0), rows(XG1, 1)

    def send_rows(copies):
        north, across, south = copies
        pl.when(not_top)(north.start)
        pl.when(is_top)(across.start)
        pl.when(not_low)(south.start)

    def wait_rows(XG, b, copies):
        north, across, south = copies
        pl.when(not_low)(north.wait_recv)

        @pl.when(is_low)
        def _():
            XG[0:3] = jnp.zeros((3, 14, 16, 128), BF)

        pl.when(not_top)(south.wait_recv)

        @pl.when(is_top)
        def _():
            across.wait_recv()
            flip = onehot(iota((224, 224), 0) + iota((224, 224), 1) == 223)
            for j in range(3):
                XG[51 + j] = dot(flip, FB[b, 2 - j].reshape(224, 128)).astype(BF).reshape(14, 16, 128)

    def insert(XG, b, ch):
        at = pl.ds(pl.multiple_of(16 * ch, 16), 16)
        o = dot(INS[...], jnp.concatenate([LH[b, at], RH[b, at]], 0)).astype(BF)
        for rr in range(R):
            row = R * ch + rr + 3
            XG[row, 0:3] = XG[row, 0:3] + o[rr * 96 : rr * 96 + 48].reshape(3, 16, 128)
            XG[row, 11:14] = XG[row, 11:14] + o[rr * 96 + 48 : rr * 96 + 96].reshape(3, 16, 128)

    def edges(b, ch, el, er):
        at = pl.ds(16 * ch if isinstance(ch, int) else pl.multiple_of(16 * ch, 16), 16)
        EL[b, at] = el.astype(BF)
        ER[b, at] = er.astype(BF)

    wet = jnp.transpose(mask[...].astype(F))

    def prep(ch):
        el = er = None
        for p in range(R // 2):
            row = R * ch + 2 * p
            both = [NAT[row + i] * jnp.broadcast_to(wet[:, row + i : row + i + 1], (COLS, C)).astype(BF) for i in range(2)]
            o = dot(G4[p], jnp.concatenate(both, 1))
            for i in range(2):
                v = o[:, C * i : C * i + C]
                XG0[row + i + 3] = v[:224].astype(BF).reshape(14, 16, 128)
                a, z = v[224 + 32 * i : 240 + 32 * i], v[240 + 32 * i : 256 + 32 * i]
                el, er = (a, z) if el is None else (el + a, er + z)
        edges(0, ch, el, er)

    def landed(copies):
        for cp in copies:
            cp.wait_recv()

    def insert_all(XG, b, lo, hi):
        def one(ch, carry):
            insert(XG, b, ch)
            return carry

        lax.fori_loop(lo, hi, one, 0)

    for i, q in enumerate((0, 3, 1, 2)):
        loads[q].wait()
        for ch in range(3 * q, 3 * q + 3):
            prep(ch)
        if i == 0:
            continue
        if i == 1:
            @pl.when(not_low)
            def _():
                pl.semaphore_wait(barrier, 4)

            @pl.when(is_low)
            def _():
                pl.semaphore_wait(barrier, 3)

        for cp in (quarters[0] if i == 1 else ()) + quarters[q]:
            cp.start()
    for cp in loads[4:]:
        cp.wait()
    for b in range(2):
        for t in range(49):
            KF[b, t] = jnp.broadcast_to(CKV[t, b : b + 1, :], (8, 128))
        W1E[b, :128] = W1V[b]
        bb = b1[b : b + 1] * HALF
        hi = bb.astype(BF).astype(F)
        lo = (bb - hi).astype(BF).astype(F)
        z = iota((128, 512), 0)
        W1E[b, 128:] = jnp.where(z == 0, hi, jnp.where(z == 1, lo, jnp.where(z == 2, bb - hi - lo, 0.0))).astype(BF)
    landed(quarters[0] + quarters[3])
    insert_all(XG0, 0, 0, 3)
    insert_all(XG0, 0, 9, 12)
    send_rows(rows0)

    def conv_stage(b, q, par):
        return conv((XG0, XG1)[b], KF.at[b], jnp.broadcast_to(cb[b : b + 1], (16, 128)), acc.at[par], R * chunk(b, q))

    def norm_stage(b, q, par, marks):
        norm(acc.at[par], nrm.at[par], gain[b : b + 1] * (HALF * 128**0.5), nb[b : b + 1] * HALF)

    def hidden_stage(b, q, par, marks):
        expand_hidden(nrm.at[par], hid.at[par], W1E.at[b], marks)

    def out_stage(b, q, par, marks):
        XG = (XG0, XG1)[b]
        ch = chunk(b, q)
        first = gate([hid[par, 16 * i : 16 * i + 16, :128] for i in range(R * 8)], marks, *SPAN[0])
        y = dot(jnp.concatenate([first, hid[par, :, 128:]], 1), W2V[b])
        y = (y + b2[b : b + 1] * (1 / HALF)) * (ls[b : b + 1] * HALF)
        xs = []
        for rr in range(R):
            row = R * ch + rr
            res = XG[row + 3, 3:11].reshape(128, 128).astype(F)
            x = (res + y[rr * 128 : rr * 128 + 128]).astype(BF)
            xs.append(x)
            if b == 0:
                XG1[row + 3, 3:11] = x.reshape(8, 16, 128)
            else:
                NAT[row] = x
        if b == 0:
            el = er = None
            for p in range(R // 2):
                o = dot(H4[p], jnp.concatenate(xs[2 * p : 2 * p + 2], 1))
                for i in range(2):
                    row = R * ch + 2 * p + i + 3
                    v = o[:, 128 * i : 128 * i + 128]
                    XG1[row, 0:3] = v[:48].astype(BF).reshape(3, 16, 128)
                    XG1[row, 11:14] = v[48:96].astype(BF).reshape(3, 16, 128)
                    a, z = v[96 + 32 * i : 112 + 32 * i], v[112 + 32 * i : 128 + 32 * i]
                    el, er = (a, z) if el is None else (el + a, er + z)
            edges(1, ch, el, er)

    def finish(ch):
        return pltpu.make_async_copy(NAT.at[pl.ds(R * ch, R)], out.at[pl.ds(R * ch, R)], out_sem.at[ch])

    stages = (out_stage, hidden_stage, norm_stage)

    def step(b, q, par):
        marks = conv_stage(b, q + 3, (par + 3) % 2)
        for d, stage in enumerate(stages):
            stage(b, q + d, (par + d) % 2, marks)

    def mixed(s):
        i = s + 3
        marks = conv_stage(i // N, i % N, i % 2) if i < 2 * N else []
        for d, stage in enumerate(stages):
            i = s + d
            if 0 <= i < 2 * N:
                stage(i // N, i % N, i % 2, marks)

    mixed(-3)
    landed(quarters[1] + quarters[2])
    insert_all(XG0, 0, 3, 9)
    mixed(-2)
    mixed(-1)

    def body0(j, carry):
        @pl.when(j == 2)
        def _():
            wait_rows(XG0, 0, rows0)
            for cp in cols_a:
                cp.start()

        step(0, 2 * j, 0)
        step(0, 2 * j + 1, 1)
        return carry

    lax.fori_loop(0, 4, body0, 0)
    for cp in cols_b:
        cp.start()
    mixed(8)
    for cp in cols_c:
        cp.start()
    landed(cols_a)
    insert_all(XG1, 1, 1, 5)
    mixed(9)
    for cp in cols_d:
        cp.start()
    mixed(10)
    landed(cols_b)
    insert_all(XG1, 1, 5, 8)
    mixed(11)
    for cp in cols_e:
        cp.start()
    landed(cols_c)
    insert(XG1, 1, 0)
    insert(XG1, 1, 11)
    send_rows(rows1)

    def body1(j, carry):
        @pl.when(j == 1)
        def _():
            landed(cols_d)
            insert(XG1, 1, 8)

        @pl.when(j == 2)
        def _():
            landed(cols_e)
            insert_all(XG1, 1, 9, 11)

        @pl.when(j == 3)
        def _():
            wait_rows(XG1, 1, rows1)

        step(1, 2 * j, 0)
        step(1, 2 * j + 1, 1)
        finish(chunk(1, 2 * j)).start()
        finish(chunk(1, 2 * j + 1)).start()
        return carry

    lax.fori_loop(0, 4, body1, 0)
    for s in range(20, 24):
        mixed(s)
        finish(chunk(1, s - N)).start()
    for cp in cols:
        cp.wait_send()
    for north, across, south in (rows0, rows1):
        pl.when(not_top)(north.wait_send)
        pl.when(is_top)(across.wait_send)
        pl.when(not_low)(south.wait_send)
    for ch in range(N):
        finish(ch).wait()


def ungroup(x, mask, out, xv, ov, mv, sem_in, sem_out):
    def fetch(q):
        return pltpu.make_async_copy(x.at[pl.ds(q * TAIL, TAIL)], xv.at[pl.ds(q * TAIL, TAIL)], sem_in.at[q])

    def put(q):
        return pltpu.make_async_copy(ov.at[pl.ds(q * TAIL, TAIL)], out.at[pl.ds(q * TAIL, TAIL)], sem_out.at[q])

    steps = ROWS // TAIL
    mask_load = pltpu.make_async_copy(mask, mv, sem_in.at[steps])
    mask_load.start()
    for q in range(steps):
        fetch(q).start()
    h, hc = iota((128, 128), 0), iota((128, 128), 1)
    order = onehot((h % 8) * 16 + h // 8 == hc)
    mask_load.wait()
    wet = jnp.transpose(mv[...].astype(F))
    for q in range(steps):
        fetch(q).wait()
        for p in range(q * TAIL, q * TAIL + TAIL, 2):
            o = dot(order, jnp.concatenate([xv[p], xv[p + 1]], 1))
            for i in range(2):
                ov[p + i] = (o[:, 128 * i : 128 * i + 128] * wet[:, p + i : p + i + 1]).astype(BF)
        put(q).start()
    for q in range(steps):
        put(q).wait()


def shards(fields, wet_mask, *w):
    CK, cb, gain, nb, W1, b1, W2, b2, ls = w
    V = pltpu.VMEM
    grouped = pl.pallas_call(
        kernel,
        out_shape=jax.ShapeDtypeStruct((ROWS, COLS, C), BF),
        in_specs=[pl.BlockSpec(memory_space=pltpu.HBM)] * 11,
        out_specs=pl.BlockSpec(memory_space=pl.ANY),
        scratch_shapes=[
            V((ROWS, COLS), jnp.int32), V((2, C), F), V((2, C), F), V((2, C), F), V((2, 512), F), V((2, C), F), V((2, C), F),
            V((ROWS, COLS, C), BF), V((54, 14, 16, C), BF), V((54, 14, 16, C), BF),
            V((49, 2, C), F), V((2, 49, 8, C), F), V((2, 128, 512), BF), V((2, 256, 512), BF), V((2, 512, 128), BF),
            V((R // 2, 288, 128), BF), V((R // 2, 160, 128), BF), V((96 * R, 32), BF),
            V((2, R * 128, C), F), V((2, R * 128, C), BF), V((2, R * 128, 512), BF),
            V((2, 192, C), BF), V((2, 192, C), BF), V((2, 192, C), BF), V((2, 192, C), BF), V((2, 3, 14, 16, C), BF),
            pltpu.SemaphoreType.DMA((14,)), pltpu.SemaphoreType.DMA((26,)), pltpu.SemaphoreType.DMA((26,)), pltpu.SemaphoreType.DMA((N,)),
        ],
        compiler_params=pltpu.CompilerParams(vmem_limit_bytes=VMB << 20, collective_id=0, has_side_effects=True),
        name="forecast",
    )(fields, wet_mask, jnp.transpose(CK, (1, 0, 2)), *w[1:])
    return pl.pallas_call(
        ungroup,
        out_shape=jax.ShapeDtypeStruct((ROWS, COLS, C), BF),
        in_specs=[pl.BlockSpec(memory_space=pl.ANY)] * 2,
        out_specs=pl.BlockSpec(memory_space=pl.ANY),
        scratch_shapes=[
            V((ROWS, COLS, C), BF), V((ROWS, COLS, C), BF), V((ROWS, COLS), jnp.int32),
            pltpu.SemaphoreType.DMA((ROWS // TAIL + 1,)), pltpu.SemaphoreType.DMA((ROWS // TAIL,)),
        ],
        compiler_params=pltpu.CompilerParams(vmem_limit_bytes=VMB << 20),
        name="ungroup",
    )(grouped, wet_mask)


def solution(mesh):
    return jax.shard_map(
        shards, mesh=mesh, in_specs=(P("lat", "lon", None), P("lat", "lon")) + (P(),) * 9,
        out_specs=P("lat", "lon", None), check_vma=False,
    )
```
